256 devices in a mesh: dp: 2 (over core), expert: 128 (over z, x, y).
Axes of the slice: x: 4, y: 4, z: 8, core: 2. Of those that a mesh axis runs over, the one named last changes fastest.
Arguments:
- out_grad: bfloat16 [16384, 1024], P(('dp', 'expert')), may hold values from -6 to 6
- layer_input: bfloat16 [16384, 1024], P(('dp', 'expert')), may hold values from -6 to 6
- combine: float32 [16384, 8], P(('dp', 'expert')), may hold values from 0.05 to 0.5
- routes: int32 [16384, 8], P(('dp', 'expert')), may hold values from 0 to 127, all different within a row; in each aligned block of 64 rows (0 to 63, 64 to 127, ...) at most 8 rows name the same one
- w_gate_up: bfloat16 [128, 1024, 768], P('expert'), may hold values from -0.1875 to 0.1875
- w_down: bfloat16 [128, 384, 1024], P('expert'), may hold values from -0.3125 to 0.3125
- m_gate_up: float32 [128, 1024, 768], P('expert', 'dp'), may hold values from -0.75 to 0.75
- v_gate_up: float32 [128, 1024, 768], P('expert', 'dp'), may hold values from 0.001 to 0.1
- m_down: float32 [128, 384, 1024], P('expert', None, 'dp'), may hold values from -0.75 to 0.75
- v_down: float32 [128, 384, 1024], P('expert', None, 'dp'), may hold values from 0.001 to 0.1
- swap_pairs: int32 [32, 2], replicated, may hold values from 0 to 127, as said below
Outputs:
- in_grad: bfloat16 [16384, 1024], P(('dp', 'expert'))
- new_gate_up: bfloat16 [128, 1024, 768], P('expert', 'dp')
- new_down: bfloat16 [128, 384, 1024], P('expert', None, 'dp')
- new_m_gate_up: float32 [128, 1024, 768], P('expert', 'dp')
- new_v_gate_up: float32 [128, 1024, 768], P('expert', 'dp')
- new_m_down: float32 [128, 384, 1024], P('expert', None, 'dp')
- new_v_down: float32 [128, 384, 1024], P('expert', None, 'dp')
The draws below stay inside these ranges and needn't reach their ends.
Inputs may be any that keep to these rules, and one draw needn't show every extreme that they name: `routes`: each row names 8 different experts; among the rows of one device no expert is named more than 8 times, a bound that some block reaches. `swap_pairs`: no device appears twice in the list; devices 0 and 127 are always in it.
All inputs are finite; a program needn't handle non-finite values. Where the reference program divides by a largest or mean magnitude, that divisor is 1e-20 or more.
Results may differ from the reference program's by a relative error of at most 0.0064.
Values may be sent and summed in bfloat16 or wider, within the bound.
A program may use at most 128 MiB of HBM per device.

```python
import functools
import math
import jax
import jax.numpy as jnp
import numpy as np
from jax import lax

D = 1024
FF = 384
TOP = 8
TOK_DEV = 64
EXPERTS = 128
CAP = 8
TOKENS = 16384
NPAIRS = 32
N_DP = 2


def draw_swap_pairs(key, part):
    middle = 1 + jax.random.permutation(jax.random.fold_in(key, 11), EXPERTS - 2)
    chosen = jnp.concatenate([jnp.array([0, EXPERTS - 1], jnp.int32), middle[:2 * NPAIRS - 2].astype(jnp.int32)])
    shuffle = jax.random.permutation(jax.random.fold_in(key, 12), 2 * NPAIRS)
    return chosen[shuffle].reshape(NPAIRS, 2).astype(jnp.int32)


def level_of(key, dims, pieces, low, top_value):
    factor_of, own = 1.0, jax.random.fold_in(key, 6)
    for dim, shards_of in pieces:
        heights = jnp.exp(jax.random.uniform(jax.random.fold_in(own, dim), (shards_of,), jnp.float32, low / len(pieces), top_value / len(pieces)))
        factor_of = factor_of * jnp.repeat(heights, dims[dim] // shards_of).reshape([-1 if axis == dim else 1 for axis in range(len(dims))])
    return factor_of


def assign_block(rng, own, number, rows, number_of, top, most, slope):
    ranking = jax.random.permutation(rng, number_of)
    packed, usual = load_shares(number_of, rows * top, most, slope, True), load_shares(number_of, rows * top, most, slope, False)
    places = jnp.arange(number_of)

    def named(tallies, offset_by):
        used = int((tallies > 0).sum())
        fixed = max(1, used // 4)
        passed = fixed + (places - fixed + offset_by * (used - fixed)) % max(1, number_of - fixed)
        return jnp.zeros((number_of,), jnp.int32).at[ranking[jnp.where(places < fixed, places, passed)]].set(jnp.asarray(tallies, jnp.int32))

    tallies = jnp.where(number % 4 == 0, named(packed, number // 4), named(usual, number - number // 4 - 1))
    mixed = jax.random.permutation(jax.random.fold_in(own, 3), number_of)
    giver, taker = mixed[0:number_of // 2 * 2:2], mixed[1:number_of // 2 * 2:2]
    slack = jnp.minimum(tallies[giver] - 1, most - tallies[taker]) // 2
    slack = jnp.where((giver == ranking[0]) | (taker == ranking[0]) | (tallies[taker] == 0), 0, jnp.maximum(slack, 0))
    passed = jax.random.randint(jax.random.fold_in(own, 4), (number_of // 2,), 0, 1 << 20) % (slack + 1)
    tallies = tallies.at[giver].add(-passed).at[taker].add(passed)
    members = jnp.searchsorted(jnp.cumsum(tallies), jnp.arange(rows * top), side="right").astype(jnp.int32)
    table = members.reshape(top, rows).T
    table = table[jax.random.permutation(jax.random.fold_in(own, 1), rows)]
    offset_by = jax.random.randint(jax.random.fold_in(own, 2), (rows, 1), 0, top)
    return jnp.take_along_axis(table, (jnp.arange(top)[None, :] + offset_by) % top, axis=1)


def load_shares(number_of, total, reach, slope, full):
    weights = [(1 << 20) // math.isqrt(standing ** slope) + 1 for standing in range(1, number_of + 1)]
    largest = reach if full else min(reach, max(-(-total // number_of), total * weights[0] // sum(weights)))
    least = 1 if total - largest >= number_of - 1 else 0
    given, rest = [largest] + [least] * (number_of - 1), total - largest - least * (number_of - 1)
    while rest > 0:
        candidates = [i for i in range(1, number_of) if given[i] < largest] or [i for i in range(1, number_of) if given[i] < reach]
        mass, budget = sum([weights[i] for i in candidates]), rest
        for i in candidates:
            extra = min(reach - given[i], max(1, budget * weights[i] // mass), rest)
            given[i] = given[i] + extra
            rest = rest - extra
    return np.array(given)


def gaussian(own_key, shape, spread, most, shards=(), held_as=jnp.bfloat16):
    result = jax.random.normal(own_key, shape, jnp.float32) * spread
    if len(shards) > 0:
        result = level_of(own_key, shape, shards, -0.22, 0.18) * result
    return jnp.clip(result, min=-most, max=most).astype(held_as)


def setup_inputs(seed: int = 0) -> dict:
    splits = jax.random.split(jax.random.key(seed), 12)
    out_grad = gaussian(splits[0], (TOKENS, D), 1.0, 6.0, ((0, 256),))
    layer_input = gaussian(splits[1], (TOKENS, D), 1.0, 6.0, ((0, 256),))
    combine = jnp.clip(jnp.exp(math.log(0.5) - 2.3025851 * jax.random.uniform(splits[2], (TOKENS, TOP), jnp.float32) ** level_of(splits[2], (TOKENS, TOP), ((0, 256),), -0.2, 0.2)), 0.05, 0.5)
    routes_keys = jax.random.split(jax.random.fold_in(splits[3], 1), TOKENS // TOK_DEV)
    routes_turns = jax.random.permutation(jax.random.fold_in(splits[3], 3), TOKENS // TOK_DEV)
    routes = jax.vmap(lambda own, number: assign_block(jax.random.fold_in(splits[3], 2), own, number, TOK_DEV, EXPERTS, TOP, CAP, 2))(routes_keys, routes_turns).reshape((TOKENS, TOP))
    w_gate_up = gaussian(splits[4], (EXPERTS, D, 2 * FF), D ** -0.5, 0.1875, ((0, 128),))
    w_down = gaussian(splits[5], (EXPERTS, FF, D), FF ** -0.5, 0.3125, ((0, 128),))
    m_gate_up = gaussian(splits[6], (EXPERTS, D, 2 * FF), 0.05, 0.75, ((0, 128), (1, 2)), jnp.float32)
    v_gate_up = jnp.clip(jnp.exp(math.log(0.1) - 4.6051702 * jax.random.uniform(splits[7], (EXPERTS, D, 2 * FF), jnp.float32) ** level_of(splits[7], (EXPERTS, D, 2 * FF), ((0, 128), (1, 2)), -0.2, 0.2)), 0.001, 0.1)
    m_down = gaussian(splits[8], (EXPERTS, FF, D), 0.05, 0.75, ((0, 128), (2, 2)), jnp.float32)
    v_down = jnp.clip(jnp.exp(math.log(0.1) - 4.6051702 * jax.random.uniform(splits[9], (EXPERTS, FF, D), jnp.float32) ** level_of(splits[9], (EXPERTS, FF, D), ((0, 128), (2, 2)), -0.2, 0.2)), 0.001, 0.1)
    swap_pairs = draw_swap_pairs(jax.random.fold_in(splits[11], 71), 0)
    return dict(out_grad=out_grad, layer_input=layer_input, combine=combine, routes=routes, w_gate_up=w_gate_up, w_down=w_down, m_gate_up=m_gate_up, v_gate_up=v_gate_up, m_down=m_down, v_down=v_down, swap_pairs=swap_pairs)


BETA_ONE = 0.9
BETA_TWO = 0.95
RATE = 0.001
DECAY = 0.1
ADAM_EPS = 1e-08
PEAK_EPS = 1e-06

def partner_table(swap_pairs, expert_count):
    devices = jnp.arange(expert_count, dtype=jnp.int32)
    first_dev = swap_pairs[:, 0]
    second_dev = swap_pairs[:, 1]
    hit_first = devices[:, None] == first_dev[None, :]
    hit_second = devices[:, None] == second_dev[None, :]
    other = lax.optimization_barrier(jnp.sum(jnp.where(hit_first, second_dev[None, :], 0) + jnp.where(hit_second, first_dev[None, :], 0), axis=1))
    paired = jnp.any(hit_first | hit_second, axis=1)
    return jnp.where(paired, other, devices).astype(jnp.int32)

def slot_ranks(route_ids, expert_count):
    flat_ids = route_ids.reshape(-1)
    onehot = (flat_ids[:, None] == jnp.arange(expert_count, dtype=jnp.int32)[None, :]).astype(jnp.int32)
    before = jnp.cumsum(onehot, axis=0) - onehot
    return lax.optimization_barrier(jnp.sum(before * onehot, axis=1)).astype(jnp.int32)

def expert_backward(slot_grad, slot_input, gate_up, down_proj):
    hidden_units = down_proj.shape[0]
    pre_act = jnp.dot(slot_input, gate_up, preferred_element_type=jnp.float32)
    gate_pre = pre_act[:, :hidden_units]
    up_pre = pre_act[:, hidden_units:]
    sigmoid_gate = jax.nn.sigmoid(gate_pre)
    gate_act = gate_pre * sigmoid_gate
    hidden = (gate_act * up_pre).astype(jnp.bfloat16)
    d_hidden = lax.dot_general(slot_grad, down_proj, (((1,), (1,)), ((), ())), preferred_element_type=jnp.float32)
    d_gate = d_hidden * up_pre * sigmoid_gate * (1.0 + gate_pre * (1.0 - sigmoid_gate))
    d_up = d_hidden * gate_act
    d_pre = jnp.concatenate([d_gate, d_up], axis=1).astype(jnp.bfloat16)
    grad_down = lax.dot_general(hidden, slot_grad, (((0,), (0,)), ((), ())), preferred_element_type=jnp.float32)
    grad_gate_up = lax.dot_general(slot_input, d_pre, (((0,), (0,)), ((), ())), preferred_element_type=jnp.float32)
    slot_back = lax.dot_general(d_pre, gate_up, (((1,), (1,)), ((), ())), preferred_element_type=jnp.float32).astype(jnp.bfloat16)
    return (slot_back, grad_gate_up, grad_down)

def adam_update(weight, grad, mean_in, square_in, scale_by):
    scaled = grad * scale_by
    mean_new = BETA_ONE * mean_in + (1.0 - BETA_ONE) * scaled
    square_new = BETA_TWO * square_in + (1.0 - BETA_TWO) * scaled * scaled
    weight_wide = weight.astype(jnp.float32)
    step_size = mean_new / (jnp.sqrt(square_new) + ADAM_EPS)
    weight_new = (weight_wide - RATE * (step_size + DECAY * weight_wide)).astype(jnp.bfloat16)
    return (weight_new, mean_new, square_new)

def reference(out_grad, layer_input, combine, routes, w_gate_up, w_down, m_gate_up, v_gate_up, m_down, v_down, swap_pairs):
    expert_count = EXPERTS
    partner = partner_table(swap_pairs, expert_count)
    assign = TOK_DEV * TOP
    blocks = N_DP * expert_count
    route_blocks = routes.reshape(blocks, TOK_DEV, TOP)
    slots = jax.vmap(functools.partial(slot_ranks, expert_count=expert_count))(route_blocks)
    route_ids = route_blocks.reshape(blocks, assign)
    block_ids = jnp.arange(blocks, dtype=jnp.int32)
    global_index = block_ids[:, None] * assign + jnp.arange(assign, dtype=jnp.int32)[None, :]
    replica_ids = jnp.broadcast_to((block_ids // expert_count)[:, None], (blocks, assign))
    source_ids = jnp.broadcast_to((block_ids % expert_count)[:, None], (blocks, assign))
    slot_owner = jnp.full((N_DP, expert_count, expert_count, CAP), -1, jnp.int32)
    slot_owner = slot_owner.at[replica_ids, route_ids, source_ids, slots].set(global_index)
    combine_flat = combine.reshape(-1)

    def scan_step(token_grad, expert):
        slot_index = lax.dynamic_index_in_dim(slot_owner, expert, 1, keepdims=False).reshape(N_DP, expert_count * CAP)
        is_live = slot_index >= 0
        safe_index = jnp.maximum(slot_index, 0)
        token_ids = safe_index // TOP
        weights = jnp.where(is_live, combine_flat[safe_index], jnp.float32(0.0))
        slot_grad = (out_grad[token_ids].astype(jnp.float32) * weights[..., None]).astype(jnp.bfloat16)
        slot_input = jnp.where(is_live[..., None], layer_input[token_ids], jnp.zeros((), jnp.bfloat16))
        gate_up = w_gate_up[expert]
        down_proj = w_down[expert]
        total_gate_up = jnp.zeros(gate_up.shape, jnp.float32)
        total_down = jnp.zeros(down_proj.shape, jnp.float32)
        for replica in range(N_DP):
            slot_back, grad_gate_up, grad_down = expert_backward(slot_grad[replica], slot_input[replica], gate_up, down_proj)
            token_grad = token_grad.at[token_ids[replica]].add(slot_back.astype(jnp.float32))
            total_gate_up = total_gate_up + grad_gate_up
            total_down = total_down + grad_down
        peak_abs = jnp.maximum(jnp.max(jnp.abs(total_gate_up)), jnp.max(jnp.abs(total_down)))
        scale_by = 1.0 / (peak_abs + PEAK_EPS)
        new_gu, gate_mean, gate_square = adam_update(gate_up, total_gate_up, m_gate_up[expert], v_gate_up[expert], scale_by)
        new_dn, down_mean, down_square = adam_update(down_proj, total_down, m_down[expert], v_down[expert], scale_by)
        return (token_grad, (new_gu, new_dn, gate_mean, gate_square, down_mean, down_square))
    start_grad = jnp.zeros((TOKENS, D), jnp.float32)
    token_grad, results = lax.scan(scan_step, start_grad, partner)
    in_grad = token_grad.astype(jnp.bfloat16)
    return (in_grad, results[0], results[1], results[2], results[3], results[4], results[5])
```

```python
import jax
import jax.numpy as jnp
from jax import lax
from jax.sharding import PartitionSpec as P

BETA_ONE = 0.9
BETA_TWO = 0.95
RATE = 0.001
DECAY = 0.1
ADAM_EPS = 1e-08
PEAK_EPS = 1e-06
SUB = 8
LANE = 128


def partner_table(swap_pairs, expert_count):
    devices = jnp.arange(expert_count, dtype=jnp.int32)
    first_dev = swap_pairs[:, 0]
    second_dev = swap_pairs[:, 1]
    hit_first = devices[:, None] == first_dev[None, :]
    hit_second = devices[:, None] == second_dev[None, :]
    other = jnp.sum(
        jnp.where(hit_first, second_dev[None, :], 0) + jnp.where(hit_second, first_dev[None, :], 0),
        axis=1,
    )
    paired = jnp.any(hit_first | hit_second, axis=1)
    return jnp.where(paired, other, devices)


def slot_select(routes, combine, expert_count, capacity):
    tok_rows = routes.shape[0]
    experts = jnp.arange(expert_count, dtype=jnp.int32)
    hit = routes[:, :, None] == experts[None, None, :]
    member = jnp.any(hit, axis=1)
    weight = jnp.sum(jnp.where(hit, combine[:, :, None], jnp.float32(0.0)), axis=1)
    earlier = jnp.tril(jnp.ones((tok_rows, tok_rows), jnp.bfloat16), -1)
    rank = jnp.dot(earlier, member.astype(jnp.bfloat16), preferred_element_type=jnp.float32)
    place = jnp.where(member, rank.astype(jnp.int32), -1)
    slots = jnp.arange(capacity, dtype=jnp.int32)
    chosen = place.T[:, None, :] == slots[None, :, None]
    slot_weight = jnp.sum(jnp.where(chosen, weight.T[:, None, :], jnp.float32(0.0)), axis=2)
    select = chosen.astype(jnp.bfloat16).reshape(expert_count * capacity, tok_rows)
    return select, slot_weight.reshape(expert_count * capacity)


def to_tiles(matrix):
    rows, cols = matrix.shape
    tiles = matrix.reshape(rows // SUB, SUB, cols // LANE, LANE).transpose(0, 2, 1, 3)
    return tiles.reshape(-1, SUB, LANE)


def from_tiles(tiles, rows, cols):
    return (
        tiles.reshape(rows // SUB, cols // LANE, SUB, LANE).transpose(0, 2, 1, 3).reshape(rows, cols)
    )


def adam_update(weight, grad, mean_in, square_in, scale_by):
    scaled = grad * scale_by
    mean_new = BETA_ONE * mean_in + (1.0 - BETA_ONE) * scaled
    square_new = BETA_TWO * square_in + (1.0 - BETA_TWO) * scaled * scaled
    weight_wide = weight.astype(jnp.float32)
    step_size = mean_new / (jnp.sqrt(square_new) + ADAM_EPS)
    weight_new = weight_wide - RATE * (step_size + DECAY * weight_wide)
    return (
        weight_new.astype(jnp.bfloat16),
        mean_new.astype(jnp.bfloat16),
        square_new.astype(jnp.bfloat16),
    )


def per_device(
    out_grad,
    layer_input,
    combine,
    routes,
    w_gate_up,
    w_down,
    m_gate_up,
    v_gate_up,
    m_down,
    v_down,
    swap_pairs,
):
    expert_count = lax.axis_size("expert")
    replicas = lax.axis_size("dp")
    replica = lax.axis_index("dp")
    partner = partner_table(swap_pairs, expert_count)
    tok_rows, top_count = routes.shape
    capacity = 2 * tok_rows * top_count // expert_count
    model_width = out_grad.shape[1]
    gate_up = w_gate_up[0]
    down_proj = w_down[0]
    hidden_units = down_proj.shape[0]

    def swap_tokens(rows):
        return lax.all_to_all(
            rows.reshape(expert_count, capacity, model_width),
            "expert",
            split_axis=0,
            concat_axis=0,
            tiled=True,
        ).reshape(expert_count * capacity, model_width)

    select, slot_weight = slot_select(routes, combine, expert_count, capacity)
    slot_input = jnp.dot(select, layer_input, preferred_element_type=jnp.float32).astype(
        jnp.bfloat16
    )
    slot_input = swap_tokens(slot_input)
    slot_grad = (
        jnp.dot(select, out_grad, preferred_element_type=jnp.float32) * slot_weight[:, None]
    ).astype(jnp.bfloat16)
    slot_grad = swap_tokens(slot_grad)

    pre_act = jnp.dot(slot_input, gate_up, preferred_element_type=jnp.float32)
    gate_pre = pre_act[:, :hidden_units]
    up_pre = pre_act[:, hidden_units:]
    sigmoid_gate = jax.nn.sigmoid(gate_pre)
    gate_act = gate_pre * sigmoid_gate
    hidden = (gate_act * up_pre).astype(jnp.bfloat16)
    d_hidden = lax.dot_general(
        slot_grad, down_proj, (((1,), (1,)), ((), ())), preferred_element_type=jnp.float32
    )
    d_gate = d_hidden * up_pre * sigmoid_gate * (1.0 + gate_pre * (1.0 - sigmoid_gate))
    d_up = d_hidden * gate_act
    d_pre = jnp.concatenate([d_gate, d_up], axis=1).astype(jnp.bfloat16)
    slot_back = lax.dot_general(
        d_pre, gate_up, (((1,), (1,)), ((), ())), preferred_element_type=jnp.float32
    ).astype(jnp.bfloat16)
    returned = swap_tokens(slot_back)
    in_grad = lax.dot_general(
        select, returned, (((0,), (0,)), ((), ())), preferred_element_type=jnp.float32
    ).astype(jnp.bfloat16)

    grad_down = lax.dot_general(
        hidden, slot_grad, (((0,), (0,)), ((), ())), preferred_element_type=jnp.float32
    )
    grad_gate_up = lax.dot_general(
        slot_input, d_pre, (((0,), (0,)), ((), ())), preferred_element_type=jnp.float32
    )
    half = model_width // replicas
    mine = replica * half
    other = (1 - replica) * half
    trade = [(0, 1), (1, 0)]
    sent_gate_up = lax.dynamic_slice_in_dim(grad_gate_up, other, half, 0).astype(jnp.bfloat16)
    sent_down = lax.dynamic_slice_in_dim(grad_down, other, half, 1).astype(jnp.bfloat16)
    part_gate_up = lax.dynamic_slice_in_dim(grad_gate_up, mine, half, 0) + lax.ppermute(
        sent_gate_up, "dp", trade
    ).astype(jnp.float32)
    part_down = lax.dynamic_slice_in_dim(grad_down, mine, half, 1) + lax.ppermute(
        sent_down, "dp", trade
    ).astype(jnp.float32)
    local_peak = jnp.maximum(jnp.max(jnp.abs(part_gate_up)), jnp.max(jnp.abs(part_down)))
    peak_abs = lax.pmax(local_peak, "dp")
    scale_by = 1.0 / (peak_abs + PEAK_EPS)
    own_gate_up = lax.dynamic_slice_in_dim(gate_up, mine, half, 0)
    own_down = lax.dynamic_slice_in_dim(down_proj, mine, half, 1)
    updated = adam_update(own_gate_up, part_gate_up, m_gate_up[0], v_gate_up[0], scale_by)
    updated += adam_update(own_down, part_down, m_down[0], v_down[0], scale_by)

    tiles = [to_tiles(u) for u in updated]
    counts = [t.shape[0] for t in tiles]
    total = sum(counts)
    per_piece = -(-total // expert_count)
    spare = per_piece * expert_count - total
    packed = jnp.concatenate(tiles + [jnp.zeros((spare, SUB, LANE), jnp.bfloat16)], axis=0)
    packed = packed.reshape(expert_count, per_piece, SUB, LANE)
    spread = lax.all_to_all(packed, "expert", split_axis=0, concat_axis=0, tiled=True)
    picked = jnp.take(spread, partner, axis=0)
    arrived = lax.all_to_all(picked, "expert", split_axis=0, concat_axis=0, tiled=True)
    arrived = arrived.reshape(-1, SUB, LANE)
    moved = []
    start = 0
    for u, count in zip(updated, counts):
        moved.append(from_tiles(arrived[start : start + count], *u.shape))
        start += count
    new_gu, gate_mean, gate_square, new_dn, down_mean, down_square = moved
    return (
        in_grad,
        new_gu[None],
        new_dn[None],
        gate_mean.astype(jnp.float32)[None],
        gate_square.astype(jnp.float32)[None],
        down_mean.astype(jnp.float32)[None],
        down_square.astype(jnp.float32)[None],
    )


def solution(mesh):
    in_specs = (
        P(("dp", "expert"), None),
        P(("dp", "expert"), None),
        P(("dp", "expert"), None),
        P(("dp", "expert"), None),
        P("expert", None, None),
        P("expert", None, None),
        P("expert", "dp", None),
        P("expert", "dp", None),
        P("expert", None, "dp"),
        P("expert", None, "dp"),
        P(),
    )
    out_specs = (
        P(("dp", "expert"), None),
        P("expert", "dp", None),
        P("expert", None, "dp"),
        P("expert", "dp", None),
        P("expert", "dp", None),
        P("expert", None, "dp"),
        P("expert", None, "dp"),
    )
    return jax.shard_map(
        per_device, mesh=mesh, in_specs=in_specs, out_specs=out_specs, check_vma=False
    )
```

```python
import jax
import jax.numpy as jnp
from jax import lax
from jax.sharding import PartitionSpec as P

BETA_ONE = 0.9
BETA_TWO = 0.95
RATE = 0.001
DECAY = 0.1
ADAM_EPS = 1e-08
PEAK_EPS = 1e-06
SUB = 8
LANE = 128


def partner_table(swap_pairs, expert_count):
    devices = jnp.arange(expert_count, dtype=jnp.int32)
    first_dev = swap_pairs[:, 0]
    second_dev = swap_pairs[:, 1]
    hit_first = devices[:, None] == first_dev[None, :]
    hit_second = devices[:, None] == second_dev[None, :]
    other = jnp.sum(
        jnp.where(hit_first, second_dev[None, :], 0) + jnp.where(hit_second, first_dev[None, :], 0),
        axis=1,
    )
    paired = jnp.any(hit_first | hit_second, axis=1)
    return jnp.where(paired, other, devices)


def slot_select(routes, combine, expert_count, capacity):
    tok_rows = routes.shape[0]
    experts = jnp.arange(expert_count, dtype=jnp.int32)
    hit = routes[:, :, None] == experts[None, None, :]
    member = jnp.any(hit, axis=1)
    weight = jnp.sum(jnp.where(hit, combine[:, :, None], jnp.float32(0.0)), axis=1)
    earlier = jnp.tril(jnp.ones((tok_rows, tok_rows), jnp.bfloat16), -1)
    rank = jnp.dot(earlier, member.astype(jnp.bfloat16), preferred_element_type=jnp.float32)
    place = jnp.where(member, rank.astype(jnp.int32), -1)
    slots = jnp.arange(capacity, dtype=jnp.int32)
    chosen = place.T[:, None, :] == slots[None, :, None]
    slot_weight = jnp.sum(jnp.where(chosen, weight.T[:, None, :], jnp.float32(0.0)), axis=2)
    select = chosen.astype(jnp.bfloat16).reshape(expert_count * capacity, tok_rows)
    return select, slot_weight.reshape(expert_count * capacity)


def to_tiles(matrix):
    rows, cols = matrix.shape
    tiles = matrix.reshape(rows // SUB, SUB, cols // LANE, LANE).transpose(0, 2, 1, 3)
    return tiles.reshape(-1, SUB, LANE)


def from_tiles(tiles, rows, cols):
    return (
        tiles.reshape(rows // SUB, cols // LANE, SUB, LANE).transpose(0, 2, 1, 3).reshape(rows, cols)
    )


def adam_update(weight, grad, mean_in, square_in, scale_by):
    scaled = grad * scale_by
    mean_new = BETA_ONE * mean_in + (1.0 - BETA_ONE) * scaled
    square_new = BETA_TWO * square_in + (1.0 - BETA_TWO) * scaled * scaled
    weight_wide = weight.astype(jnp.float32)
    step_size = mean_new / (jnp.sqrt(square_new) + ADAM_EPS)
    weight_new = weight_wide - RATE * (step_size + DECAY * weight_wide)
    return (
        weight_new.astype(jnp.bfloat16),
        mean_new.astype(jnp.bfloat16),
        square_new.astype(jnp.bfloat16),
    )


def per_device(
    out_grad,
    layer_input,
    combine,
    routes,
    w_gate_up,
    w_down,
    m_gate_up,
    v_gate_up,
    m_down,
    v_down,
    swap_pairs,
):
    expert_count = lax.axis_size("expert")
    replicas = lax.axis_size("dp")
    replica = lax.axis_index("dp")
    partner = partner_table(swap_pairs, expert_count)
    tok_rows, top_count = routes.shape
    capacity = 2 * tok_rows * top_count // expert_count
    model_width = out_grad.shape[1]
    gate_up = w_gate_up[0]
    down_proj = w_down[0]
    hidden_units = down_proj.shape[0]

    def swap_tokens(rows):
        return lax.all_to_all(
            rows.reshape(expert_count, capacity, model_width),
            "expert",
            split_axis=0,
            concat_axis=0,
            tiled=True,
        ).reshape(expert_count * capacity, model_width)

    select, slot_weight = slot_select(routes, combine, expert_count, capacity)
    slot_input = jnp.dot(select, layer_input, preferred_element_type=jnp.float32).astype(
        jnp.bfloat16
    )
    slot_input = swap_tokens(slot_input)
    slot_grad = (
        jnp.dot(select, out_grad, preferred_element_type=jnp.float32) * slot_weight[:, None]
    ).astype(jnp.bfloat16)
    slot_grad = swap_tokens(slot_grad)

    pre_act = jnp.dot(slot_input, gate_up, preferred_element_type=jnp.float32)
    gate_pre = pre_act[:, :hidden_units]
    up_pre = pre_act[:, hidden_units:]
    sigmoid_gate = jax.nn.sigmoid(gate_pre)
    gate_act = gate_pre * sigmoid_gate
    hidden = (gate_act * up_pre).astype(jnp.bfloat16)
    d_hidden = lax.dot_general(
        slot_grad, down_proj, (((1,), (1,)), ((), ())), preferred_element_type=jnp.float32
    )
    d_gate = d_hidden * up_pre * sigmoid_gate * (1.0 + gate_pre * (1.0 - sigmoid_gate))
    d_up = d_hidden * gate_act
    d_pre = jnp.concatenate([d_gate, d_up], axis=1).astype(jnp.bfloat16)
    slot_back = lax.dot_general(
        d_pre, gate_up, (((1,), (1,)), ((), ())), preferred_element_type=jnp.float32
    ).astype(jnp.bfloat16)
    slot_back, d_pre, hidden = lax.optimization_barrier((slot_back, d_pre, hidden))
    returned = swap_tokens(slot_back)

    grad_down = lax.dot_general(
        hidden, slot_grad, (((0,), (0,)), ((), ())), preferred_element_type=jnp.float32
    )
    grad_gate_up = lax.dot_general(
        slot_input, d_pre, (((0,), (0,)), ((), ())), preferred_element_type=jnp.float32
    )
    half = model_width // replicas
    mine = replica * half
    other = (1 - replica) * half
    trade = [(0, 1), (1, 0)]
    sent_gate_up = lax.dynamic_slice_in_dim(grad_gate_up, other, half, 0).astype(jnp.bfloat16)
    sent_down = lax.dynamic_slice_in_dim(grad_down, other, half, 1).astype(jnp.bfloat16)
    part_gate_up = lax.dynamic_slice_in_dim(grad_gate_up, mine, half, 0) + lax.ppermute(
        sent_gate_up, "dp", trade
    ).astype(jnp.float32)
    part_down = lax.dynamic_slice_in_dim(grad_down, mine, half, 1) + lax.ppermute(
        sent_down, "dp", trade
    ).astype(jnp.float32)
    local_peak = jnp.maximum(jnp.max(jnp.abs(part_gate_up)), jnp.max(jnp.abs(part_down)))
    peak_abs = lax.pmax(local_peak, "dp")
    scale_by = 1.0 / (peak_abs + PEAK_EPS)
    own_gate_up = lax.dynamic_slice_in_dim(gate_up, mine, half, 0)
    own_down = lax.dynamic_slice_in_dim(down_proj, mine, half, 1)
    updated = adam_update(own_gate_up, part_gate_up, m_gate_up[0], v_gate_up[0], scale_by)
    updated += adam_update(own_down, part_down, m_down[0], v_down[0], scale_by)

    tiles = [to_tiles(u) for u in updated]
    counts = [t.shape[0] for t in tiles]
    total = sum(counts)
    per_piece = -(-total // expert_count)
    spare = per_piece * expert_count - total
    packed = jnp.concatenate(tiles + [jnp.zeros((spare, SUB, LANE), jnp.bfloat16)], axis=0)
    packed = packed.reshape(expert_count, per_piece, SUB, LANE)
    packed, returned = lax.optimization_barrier((packed, returned))
    spread = lax.all_to_all(packed, "expert", split_axis=0, concat_axis=0, tiled=True)
    in_grad = lax.dot_general(
        select, returned, (((0,), (0,)), ((), ())), preferred_element_type=jnp.float32
    ).astype(jnp.bfloat16)
    picked = spread.at[partner].get(mode="promise_in_bounds")
    arrived = lax.all_to_all(picked, "expert", split_axis=0, concat_axis=0, tiled=True)
    arrived = arrived.reshape(-1, SUB, LANE)
    moved = []
    start = 0
    for u, count in zip(updated, counts):
        moved.append(from_tiles(arrived[start : start + count], *u.shape))
        start += count
    new_gu, gate_mean, gate_square, new_dn, down_mean, down_square = moved
    return (
        in_grad,
        new_gu[None],
        new_dn[None],
        gate_mean.astype(jnp.float32)[None],
        gate_square.astype(jnp.float32)[None],
        down_mean.astype(jnp.float32)[None],
        down_square.astype(jnp.float32)[None],
    )


def solution(mesh):
    in_specs = (
        P(("dp", "expert"), None),
        P(("dp", "expert"), None),
        P(("dp", "expert"), None),
        P(("dp", "expert"), None),
        P("expert", None, None),
        P("expert", None, None),
        P("expert", "dp", None),
        P("expert", "dp", None),
        P("expert", None, "dp"),
        P("expert", None, "dp"),
        P(),
    )
    out_specs = (
        P(("dp", "expert"), None),
        P("expert", "dp", None),
        P("expert", None, "dp"),
        P("expert", "dp", None),
        P("expert", "dp", None),
        P("expert", None, "dp"),
        P("expert", None, "dp"),
    )
    return jax.shard_map(
        per_device, mesh=mesh, in_specs=in_specs, out_specs=out_specs, check_vma=False
    )
```

```python
import functools

import jax
import jax.numpy as jnp
from jax import lax
from jax.experimental import pallas as pl
from jax.experimental.pallas import tpu as pltpu
from jax.sharding import PartitionSpec as P

BETA_ONE = 0.9
BETA_TWO = 0.95
RATE = 0.001
DECAY = 0.1
ADAM_EPS = 1e-08
PEAK_EPS = 1e-06
SUB = 8
LANE = 128
PLANE = 16


def partner_table(swap_pairs, expert_count):
    devices = jnp.arange(expert_count, dtype=jnp.int32)
    first_dev = swap_pairs[:, 0]
    second_dev = swap_pairs[:, 1]
    hit_first = devices[:, None] == first_dev[None, :]
    hit_second = devices[:, None] == second_dev[None, :]
    other = jnp.sum(
        jnp.where(hit_first, second_dev[None, :], 0) + jnp.where(hit_second, first_dev[None, :], 0),
        axis=1,
    )
    paired = jnp.any(hit_first | hit_second, axis=1)
    return jnp.where(paired, other, devices)


def home_select(routes, expert_count, capacity):
    tok_rows = routes.shape[0]
    experts = jnp.arange(expert_count, dtype=jnp.int32)
    member = jnp.any(routes[:, :, None] == experts[None, None, :], axis=1)
    earlier = jnp.tril(jnp.ones((tok_rows, tok_rows), jnp.bfloat16), -1)
    rank = jnp.dot(earlier, member.astype(jnp.bfloat16), preferred_element_type=jnp.float32)
    place = jnp.where(member, rank.astype(jnp.int32), -1)
    slots = jnp.arange(capacity, dtype=jnp.int32)
    chosen = place.T[:, None, :] == slots[None, :, None]
    return chosen.astype(jnp.bfloat16).reshape(expert_count * capacity, tok_rows)


def column_select(routes, combine, first_expert, plane, sources, capacity):
    top_count, columns = routes.shape
    tok_rows = columns // sources
    wanted = first_expert + jnp.arange(plane, dtype=jnp.int32)
    hit = routes[:, None, :] == wanted[None, :, None]
    member = jnp.any(hit, axis=0)
    weight = jnp.sum(jnp.where(hit, combine[:, None, :], jnp.float32(0.0)), axis=0)
    column = jnp.arange(columns, dtype=jnp.int32)
    source = column // tok_rows
    earlier = (column[:, None] < column[None, :]) & (source[:, None] == source[None, :])
    rank = jnp.dot(
        member.astype(jnp.bfloat16),
        earlier.astype(jnp.bfloat16),
        preferred_element_type=jnp.float32,
    )
    code = jnp.where(member, source[None, :] * capacity + rank.astype(jnp.int32), -1)
    slots = jnp.arange(sources * capacity, dtype=jnp.int32)
    chosen = code[:, None, :] == slots[None, :, None]
    slot_weight = jnp.sum(jnp.where(chosen, weight[:, None, :], jnp.float32(0.0)), axis=2)
    select = chosen.astype(jnp.bfloat16).reshape(plane * sources * capacity, columns)
    return select, slot_weight.reshape(-1)


def ring_kernel(depth, plane, *refs):
    ins = refs[:3]
    outs = refs[3:6]
    send_sem, recv_sem = refs[6:]
    me = lax.axis_index("expert")
    layer = me // plane
    spot = me % plane
    ahead = ((layer + 1) % depth) * plane + spot
    behind = ((layer + depth - 1) % depth) * plane + spot
    targets = (ahead, behind)

    barrier = pltpu.get_barrier_semaphore()
    for target in targets:
        pl.semaphore_signal(
            barrier, inc=1, device_id={"expert": target}, device_id_type=pl.DeviceIdType.MESH
        )
    pl.semaphore_wait(barrier, 2)

    half = depth // 2

    def copy_of(way, step, which):
        if way == 0:
            block = (layer + depth - step) % depth
        else:
            block = (layer + step) % depth
        source = ins[which] if step == 0 else outs[which].at[block]
        return pltpu.make_async_remote_copy(
            src_ref=source,
            dst_ref=outs[which].at[block],
            send_sem=send_sem.at[way, step, which],
            recv_sem=recv_sem.at[way, step, which],
            device_id={"expert": targets[way]},
            device_id_type=pl.DeviceIdType.MESH,
        )

    started = []
    previous = {}
    for step in range(half):
        for which in (2, 0, 1):
            for way in (0, 1):
                if step == half - 1 and way != (0 if which == 0 else 1):
                    continue
                if step > 0:
                    previous[(way, which)].wait_recv()
                    previous.pop((way, which))
                copy = copy_of(way, step, which)
                copy.start()
                started.append(copy)
                previous[(way, which)] = copy
        if step == 0:
            for which in range(3):
                outs[which][layer] = ins[which][...]
    for copy in previous.values():
        copy.wait_recv()
    for copy in started:
        copy.wait_send()


def gather_column(arrays, depth, plane):
    half = depth // 2
    return pl.pallas_call(
        functools.partial(ring_kernel, depth, plane),
        out_shape=[jax.ShapeDtypeStruct((depth,) + a.shape, a.dtype) for a in arrays],
        in_specs=[pl.BlockSpec(memory_space=pltpu.VMEM)] * 3,
        out_specs=[pl.BlockSpec(memory_space=pltpu.VMEM)] * 3,
        scratch_shapes=[
            pltpu.SemaphoreType.DMA((2, half, 3)),
            pltpu.SemaphoreType.DMA((2, half, 3)),
        ],
        compiler_params=pltpu.CompilerParams(
            collective_id=0, has_side_effects=True, vmem_limit_bytes=16 * 1024 * 1024
        ),
    )(*arrays)


def to_tiles(matrix):
    rows, cols = matrix.shape
    tiles = matrix.reshape(rows // SUB, SUB, cols // LANE, LANE).transpose(0, 2, 1, 3)
    return tiles.reshape(-1, SUB, LANE)


def from_tiles(tiles, rows, cols):
    return (
        tiles.reshape(rows // SUB, cols // LANE, SUB, LANE).transpose(0, 2, 1, 3).reshape(rows, cols)
    )


def adam_update(weight, grad, mean_in, square_in, scale_by):
    scaled = grad * scale_by
    mean_new = BETA_ONE * mean_in + (1.0 - BETA_ONE) * scaled
    square_new = BETA_TWO * square_in + (1.0 - BETA_TWO) * scaled * scaled
    weight_wide = weight.astype(jnp.float32)
    step_size = mean_new / (jnp.sqrt(square_new) + ADAM_EPS)
    weight_new = weight_wide - RATE * (step_size + DECAY * weight_wide)
    return (
        weight_new.astype(jnp.bfloat16),
        mean_new.astype(jnp.bfloat16),
        square_new.astype(jnp.bfloat16),
    )


def per_device(
    out_grad,
    layer_input,
    combine,
    routes,
    w_gate_up,
    w_down,
    m_gate_up,
    v_gate_up,
    m_down,
    v_down,
    swap_pairs,
):
    expert_count = lax.axis_size("expert")
    replicas = lax.axis_size("dp")
    replica = lax.axis_index("dp")
    partner = partner_table(swap_pairs, expert_count)
    tok_rows, top_count = routes.shape
    capacity = 2 * tok_rows * top_count // expert_count
    model_width = out_grad.shape[1]
    gate_up = w_gate_up[0]
    down_proj = w_down[0]
    hidden_units = down_proj.shape[0]

    def swap_tokens(rows):
        return lax.all_to_all(
            rows.reshape(expert_count, capacity, model_width),
            "expert",
            split_axis=0,
            concat_axis=0,
            tiled=True,
        ).reshape(expert_count * capacity, model_width)

    plane = PLANE
    depth = expert_count // plane
    layer = lax.axis_index("expert") // plane
    groups = [[z * plane + spot for spot in range(plane)] for z in range(depth)]

    def send_in_plane(rows):
        return lax.all_to_all(
            rows.reshape(plane, depth * capacity, model_width),
            "expert",
            split_axis=0,
            concat_axis=0,
            axis_index_groups=groups,
            tiled=True,
        ).reshape(expert_count * capacity, model_width)

    notes = jnp.concatenate([routes.T.astype(jnp.float32), combine.T], axis=0)
    notes = jnp.pad(notes, ((0, 0), (0, LANE - tok_rows)))
    all_input, all_grad, all_notes = gather_column((layer_input, out_grad, notes), depth, plane)
    all_notes = all_notes[:, :, :tok_rows].transpose(1, 0, 2).reshape(2 * top_count, -1)
    column_routes = all_notes[:top_count].astype(jnp.int32)
    pick, slot_weight = column_select(
        column_routes, all_notes[top_count:], layer * plane, plane, depth, capacity
    )
    slot_input = jnp.dot(
        pick, all_input.reshape(-1, model_width), preferred_element_type=jnp.float32
    ).astype(jnp.bfloat16)
    slot_input = send_in_plane(slot_input)
    slot_grad = (
        jnp.dot(pick, all_grad.reshape(-1, model_width), preferred_element_type=jnp.float32)
        * slot_weight[:, None]
    ).astype(jnp.bfloat16)
    slot_grad = send_in_plane(slot_grad)
    select = home_select(routes, expert_count, capacity)

    pre_act = jnp.dot(slot_input, gate_up, preferred_element_type=jnp.float32)
    gate_pre = pre_act[:, :hidden_units]
    up_pre = pre_act[:, hidden_units:]
    sigmoid_gate = jax.nn.sigmoid(gate_pre)
    gate_act = gate_pre * sigmoid_gate
    hidden = (gate_act * up_pre).astype(jnp.bfloat16)
    d_hidden = lax.dot_general(
        slot_grad, down_proj, (((1,), (1,)), ((), ())), preferred_element_type=jnp.float32
    )
    d_gate = d_hidden * up_pre * sigmoid_gate * (1.0 + gate_pre * (1.0 - sigmoid_gate))
    d_up = d_hidden * gate_act
    d_pre = jnp.concatenate([d_gate, d_up], axis=1).astype(jnp.bfloat16)
    slot_back = lax.dot_general(
        d_pre, gate_up, (((1,), (1,)), ((), ())), preferred_element_type=jnp.float32
    ).astype(jnp.bfloat16)
    slot_back, d_pre, hidden = lax.optimization_barrier((slot_back, d_pre, hidden))
    by_home = slot_back.reshape(plane, depth, capacity, model_width).transpose(1, 0, 2, 3)
    returned = swap_tokens(by_home)

    grad_down = lax.dot_general(
        hidden, slot_grad, (((0,), (0,)), ((), ())), preferred_element_type=jnp.float32
    )
    grad_gate_up = lax.dot_general(
        slot_input, d_pre, (((0,), (0,)), ((), ())), preferred_element_type=jnp.float32
    )
    half = model_width // replicas
    mine = replica * half
    other = (1 - replica) * half
    trade = [(0, 1), (1, 0)]
    sent_gate_up = lax.dynamic_slice_in_dim(grad_gate_up, other, half, 0).astype(jnp.bfloat16)
    sent_down = lax.dynamic_slice_in_dim(grad_down, other, half, 1).astype(jnp.bfloat16)
    part_gate_up = lax.dynamic_slice_in_dim(grad_gate_up, mine, half, 0) + lax.ppermute(
        sent_gate_up, "dp", trade
    ).astype(jnp.float32)
    part_down = lax.dynamic_slice_in_dim(grad_down, mine, half, 1) + lax.ppermute(
        sent_down, "dp", trade
    ).astype(jnp.float32)
    local_peak = jnp.maximum(jnp.max(jnp.abs(part_gate_up)), jnp.max(jnp.abs(part_down)))
    peak_abs = lax.pmax(local_peak, "dp")
    scale_by = 1.0 / (peak_abs + PEAK_EPS)
    own_gate_up = lax.dynamic_slice_in_dim(gate_up, mine, half, 0)
    own_down = lax.dynamic_slice_in_dim(down_proj, mine, half, 1)
    updated = adam_update(own_gate_up, part_gate_up, m_gate_up[0], v_gate_up[0], scale_by)
    updated += adam_update(own_down, part_down, m_down[0], v_down[0], scale_by)

    tiles = [to_tiles(u) for u in updated]
    counts = [t.shape[0] for t in tiles]
    total = sum(counts)
    per_piece = -(-total // expert_count)
    spare = per_piece * expert_count - total
    packed = jnp.concatenate(tiles + [jnp.zeros((spare, SUB, LANE), jnp.bfloat16)], axis=0)
    packed = packed.reshape(expert_count, per_piece, SUB, LANE)
    packed, returned = lax.optimization_barrier((packed, returned))
    spread = lax.all_to_all(packed, "expert", split_axis=0, concat_axis=0, tiled=True)
    in_grad = lax.dot_general(
        select, returned, (((0,), (0,)), ((), ())), preferred_element_type=jnp.float32
    ).astype(jnp.bfloat16)
    picked = spread.at[partner].get(mode="promise_in_bounds")
    arrived = lax.all_to_all(picked, "expert", split_axis=0, concat_axis=0, tiled=True)
    arrived = arrived.reshape(-1, SUB, LANE)
    moved = []
    start = 0
    for u, count in zip(updated, counts):
        moved.append(from_tiles(arrived[start : start + count], *u.shape))
        start += count
    new_gu, gate_mean, gate_square, new_dn, down_mean, down_square = moved
    return (
        in_grad,
        new_gu[None],
        new_dn[None],
        gate_mean.astype(jnp.float32)[None],
        gate_square.astype(jnp.float32)[None],
        down_mean.astype(jnp.float32)[None],
        down_square.astype(jnp.float32)[None],
    )


def solution(mesh):
    in_specs = (
        P(("dp", "expert"), None),
        P(("dp", "expert"), None),
        P(("dp", "expert"), None),
        P(("dp", "expert"), None),
        P("expert", None, None),
        P("expert", None, None),
        P("expert", "dp", None),
        P("expert", "dp", None),
        P("expert", None, "dp"),
        P("expert", None, "dp"),
        P(),
    )
    out_specs = (
        P(("dp", "expert"), None),
        P("expert", "dp", None),
        P("expert", None, "dp"),
        P("expert", "dp", None),
        P("expert", "dp", None),
        P("expert", None, "dp"),
        P("expert", None, "dp"),
    )
    return jax.shard_map(
        per_device, mesh=mesh, in_specs=in_specs, out_specs=out_specs, check_vma=False
    )
```

```python
import functools

import jax
import jax.numpy as jnp
from jax import lax
from jax.experimental import pallas as pl
from jax.experimental.pallas import tpu as pltpu
from jax.sharding import PartitionSpec as P

BETA_ONE = 0.9
BETA_TWO = 0.95
RATE = 0.001
DECAY = 0.1
ADAM_EPS = 1e-08
PEAK_EPS = 1e-06
SUB = 8
LANE = 128
PLANE = 16


def partner_table(swap_pairs, expert_count):
    devices = jnp.arange(expert_count, dtype=jnp.int32)
    first_dev = swap_pairs[:, 0]
    second_dev = swap_pairs[:, 1]
    hit_first = devices[:, None] == first_dev[None, :]
    hit_second = devices[:, None] == second_dev[None, :]
    other = jnp.sum(
        jnp.where(hit_first, second_dev[None, :], 0) + jnp.where(hit_second, first_dev[None, :], 0),
        axis=1,
    )
    paired = jnp.any(hit_first | hit_second, axis=1)
    return jnp.where(paired, other, devices)


def home_select(routes, expert_count, capacity):
    tok_rows = routes.shape[0]
    experts = jnp.arange(expert_count, dtype=jnp.int32)
    member = jnp.any(routes[:, :, None] == experts[None, None, :], axis=1)
    earlier = jnp.tril(jnp.ones((tok_rows, tok_rows), jnp.bfloat16), -1)
    rank = jnp.dot(earlier, member.astype(jnp.bfloat16), preferred_element_type=jnp.float32)
    place = jnp.where(member, rank.astype(jnp.int32), -1)
    slots = jnp.arange(capacity, dtype=jnp.int32)
    chosen = place.T[:, None, :] == slots[None, :, None]
    return chosen.astype(jnp.bfloat16).reshape(expert_count * capacity, tok_rows)


def column_select(routes, combine, first_expert, plane, sources, capacity):
    top_count, columns = routes.shape
    tok_rows = columns // sources
    wanted = first_expert + jnp.arange(plane, dtype=jnp.int32)
    hit = routes[:, None, :] == wanted[None, :, None]
    member = jnp.any(hit, axis=0)
    weight = jnp.sum(jnp.where(hit, combine[:, None, :], jnp.float32(0.0)), axis=0)
    column = jnp.arange(columns, dtype=jnp.int32)
    source = column // tok_rows
    earlier = (column[:, None] < column[None, :]) & (source[:, None] == source[None, :])
    rank = jnp.dot(
        member.astype(jnp.bfloat16),
        earlier.astype(jnp.bfloat16),
        preferred_element_type=jnp.float32,
    )
    code = jnp.where(member, source[None, :] * capacity + rank.astype(jnp.int32), -1)
    slots = jnp.arange(sources * capacity, dtype=jnp.int32)
    chosen = code[:, None, :] == slots[None, :, None]
    slot_weight = jnp.sum(jnp.where(chosen, weight[:, None, :], jnp.float32(0.0)), axis=2)
    select = chosen.astype(jnp.bfloat16).reshape(plane * sources * capacity, columns)
    return select, slot_weight.reshape(-1)


def ring_kernel(depth, plane, count, *refs):
    ins = refs[:count]
    outs = refs[count : 2 * count]
    send_sem, recv_sem = refs[2 * count :]
    me = lax.axis_index("expert")
    layer = me // plane
    spot = me % plane
    ahead = ((layer + 1) % depth) * plane + spot
    behind = ((layer + depth - 1) % depth) * plane + spot
    targets = (ahead, behind)

    barrier = pltpu.get_barrier_semaphore()
    for target in targets:
        pl.semaphore_signal(
            barrier, inc=1, device_id={"expert": target}, device_id_type=pl.DeviceIdType.MESH
        )
    pl.semaphore_wait(barrier, 2)

    half = depth // 2

    def copy_of(way, step, which):
        if way == 0:
            block = (layer + depth - step) % depth
        else:
            block = (layer + step) % depth
        source = ins[which] if step == 0 else outs[which].at[block]
        target = outs[which].at[block]
        if step == half - 1:
            rows = ins[which].shape[0] // 2
            source = source.at[pl.ds(way * rows, rows)]
            target = target.at[pl.ds(way * rows, rows)]
        return pltpu.make_async_remote_copy(
            src_ref=source,
            dst_ref=target,
            send_sem=send_sem.at[way, step, which],
            recv_sem=recv_sem.at[way, step, which],
            device_id={"expert": targets[way]},
            device_id_type=pl.DeviceIdType.MESH,
        )

    started = []
    previous = {}
    for step in range(half):
        for which in range(count):
            for way in (0, 1):
                if step > 0:
                    previous[(way, which)].wait_recv()
                copy = copy_of(way, step, which)
                copy.start()
                started.append(copy)
                previous[(way, which)] = copy
        if step == 0:
            for which in range(count):
                outs[which][layer] = ins[which][...]
    for copy in previous.values():
        copy.wait_recv()
    for copy in started:
        copy.wait_send()


def gather_column(arrays, depth, plane, collective_id):
    half = depth // 2
    count = len(arrays)
    moved = sum(a.size * a.dtype.itemsize for a in arrays) * depth
    return pl.pallas_call(
        functools.partial(ring_kernel, depth, plane, count),
        out_shape=[jax.ShapeDtypeStruct((depth,) + a.shape, a.dtype) for a in arrays],
        in_specs=[pl.BlockSpec(memory_space=pltpu.VMEM)] * count,
        out_specs=[pl.BlockSpec(memory_space=pltpu.VMEM)] * count,
        scratch_shapes=[
            pltpu.SemaphoreType.DMA((2, half, count)),
            pltpu.SemaphoreType.DMA((2, half, count)),
        ],
        compiler_params=pltpu.CompilerParams(
            collective_id=collective_id,
            has_side_effects=True,
            vmem_limit_bytes=16 * 1024 * 1024,
        ),
        cost_estimate=pl.CostEstimate(flops=0, bytes_accessed=40 * moved, transcendentals=0),
    )(*arrays)


UNPACK_STEPS = 8


def unpack_kernel(*refs):
    for tiles, out in zip(refs[:6], refs[6:]):
        cols = out.shape[1] // LANE
        for group in range(out.shape[0] // SUB):
            for col in range(cols):
                out[group * SUB : (group + 1) * SUB, col * LANE : (col + 1) * LANE] = tiles[
                    group * cols + col
                ].astype(out.dtype)


def unpack_tiles(arrived, shapes, dtypes):
    in_specs = []
    out_specs = []
    start = 0
    for rows, cols in shapes:
        count = rows * cols // (SUB * LANE)
        block = count // UNPACK_STEPS
        first = start // block
        in_specs.append(
            pl.BlockSpec((block, SUB, LANE), functools.partial(lambda b, i: (b + i, 0, 0), first))
        )
        out_specs.append(pl.BlockSpec((rows // UNPACK_STEPS, cols), lambda i: (i, 0)))
        start += count
    return pl.pallas_call(
        unpack_kernel,
        grid=(UNPACK_STEPS,),
        out_shape=[jax.ShapeDtypeStruct(s, d) for s, d in zip(shapes, dtypes)],
        in_specs=in_specs,
        out_specs=out_specs,
    )(*([arrived] * 6))


def to_tiles(matrix):
    rows, cols = matrix.shape
    tiles = matrix.reshape(rows // SUB, SUB, cols // LANE, LANE).transpose(0, 2, 1, 3)
    return tiles.reshape(-1, SUB, LANE)


def adam_update(weight, grad, mean_in, square_in, scale_by):
    scaled = grad * scale_by
    mean_new = BETA_ONE * mean_in + (1.0 - BETA_ONE) * scaled
    square_new = BETA_TWO * square_in + (1.0 - BETA_TWO) * scaled * scaled
    weight_wide = weight.astype(jnp.float32)
    step_size = mean_new / (jnp.sqrt(square_new) + ADAM_EPS)
    weight_new = weight_wide - RATE * (step_size + DECAY * weight_wide)
    return (
        weight_new.astype(jnp.bfloat16),
        mean_new.astype(jnp.bfloat16),
        square_new.astype(jnp.bfloat16),
    )


def per_device(
    out_grad,
    layer_input,
    combine,
    routes,
    w_gate_up,
    w_down,
    m_gate_up,
    v_gate_up,
    m_down,
    v_down,
    swap_pairs,
):
    expert_count = lax.axis_size("expert")
    replicas = lax.axis_size("dp")
    replica = lax.axis_index("dp")
    partner = partner_table(swap_pairs, expert_count)
    tok_rows, top_count = routes.shape
    capacity = 2 * tok_rows * top_count // expert_count
    model_width = out_grad.shape[1]
    gate_up = w_gate_up[0]
    down_proj = w_down[0]
    hidden_units = down_proj.shape[0]

    def swap_tokens(rows):
        return lax.all_to_all(
            rows.reshape(expert_count, capacity, model_width),
            "expert",
            split_axis=0,
            concat_axis=0,
            tiled=True,
        ).reshape(expert_count * capacity, model_width)

    plane = PLANE
    depth = expert_count // plane
    layer = lax.axis_index("expert") // plane
    groups = [[z * plane + spot for spot in range(plane)] for z in range(depth)]

    def send_in_plane(rows):
        return lax.all_to_all(
            rows.reshape(plane, depth * capacity, model_width),
            "expert",
            split_axis=0,
            concat_axis=0,
            axis_index_groups=groups,
            tiled=True,
        ).reshape(expert_count * capacity, model_width)

    notes = jnp.concatenate([routes.T.astype(jnp.float32), combine.T], axis=0)
    notes = jnp.pad(notes, ((0, 0), (0, LANE - tok_rows)))
    all_notes, all_input = gather_column((notes, layer_input), depth, plane, 0)
    all_notes = all_notes[:, :, :tok_rows].transpose(1, 0, 2).reshape(2 * top_count, -1)
    column_routes = all_notes[:top_count].astype(jnp.int32)
    pick, slot_weight = column_select(
        column_routes, all_notes[top_count:], layer * plane, plane, depth, capacity
    )
    slot_input = jnp.dot(
        pick, all_input.reshape(-1, model_width), preferred_element_type=jnp.float32
    ).astype(jnp.bfloat16)
    slot_input, out_grad = lax.optimization_barrier((slot_input, out_grad))
    slot_input = send_in_plane(slot_input)
    (all_grad,) = gather_column((out_grad,), depth, plane, 1)
    slot_grad = (
        jnp.dot(pick, all_grad.reshape(-1, model_width), preferred_element_type=jnp.float32)
        * slot_weight[:, None]
    ).astype(jnp.bfloat16)
    slot_grad = send_in_plane(slot_grad)
    select = home_select(routes, expert_count, capacity)

    pre_act = jnp.dot(slot_input, gate_up, preferred_element_type=jnp.float32)
    gate_pre = pre_act[:, :hidden_units]
    up_pre = pre_act[:, hidden_units:]
    sigmoid_gate = jax.nn.sigmoid(gate_pre)
    gate_act = gate_pre * sigmoid_gate
    hidden = (gate_act * up_pre).astype(jnp.bfloat16)
    d_hidden = lax.dot_general(
        slot_grad, down_proj, (((1,), (1,)), ((), ())), preferred_element_type=jnp.float32
    )
    d_gate = d_hidden * up_pre * sigmoid_gate * (1.0 + gate_pre * (1.0 - sigmoid_gate))
    d_up = d_hidden * gate_act
    d_pre = jnp.concatenate([d_gate, d_up], axis=1).astype(jnp.bfloat16)
    slot_back = lax.dot_general(
        d_pre, gate_up, (((1,), (1,)), ((), ())), preferred_element_type=jnp.float32
    ).astype(jnp.bfloat16)
    slot_back, d_pre, hidden = lax.optimization_barrier((slot_back, d_pre, hidden))
    by_home = slot_back.reshape(plane, depth, capacity, model_width).transpose(1, 0, 2, 3)
    returned = swap_tokens(by_home)

    grad_down = lax.dot_general(
        hidden, slot_grad, (((0,), (0,)), ((), ())), preferred_element_type=jnp.float32
    )
    grad_gate_up = lax.dot_general(
        slot_input, d_pre, (((0,), (0,)), ((), ())), preferred_element_type=jnp.float32
    )
    half = model_width // replicas
    mine = replica * half
    other = (1 - replica) * half
    trade = [(0, 1), (1, 0)]
    sent_gate_up = lax.dynamic_slice_in_dim(grad_gate_up, other, half, 0).astype(jnp.bfloat16)
    sent_down = lax.dynamic_slice_in_dim(grad_down, other, half, 1).astype(jnp.bfloat16)
    part_gate_up = lax.dynamic_slice_in_dim(grad_gate_up, mine, half, 0) + lax.ppermute(
        sent_gate_up, "dp", trade
    ).astype(jnp.float32)
    part_down = lax.dynamic_slice_in_dim(grad_down, mine, half, 1) + lax.ppermute(
        sent_down, "dp", trade
    ).astype(jnp.float32)
    local_peak = jnp.maximum(jnp.max(jnp.abs(part_gate_up)), jnp.max(jnp.abs(part_down)))
    peak_abs = lax.pmax(local_peak, "dp")
    scale_by = 1.0 / (peak_abs + PEAK_EPS)
    own_gate_up = lax.dynamic_slice_in_dim(gate_up, mine, half, 0)
    own_down = lax.dynamic_slice_in_dim(down_proj, mine, half, 1)
    updated = adam_update(own_gate_up, part_gate_up, m_gate_up[0], v_gate_up[0], scale_by)
    updated += adam_update(own_down, part_down, m_down[0], v_down[0], scale_by)

    tiles = [to_tiles(u) for u in updated]
    counts = [t.shape[0] for t in tiles]
    total = sum(counts)
    per_piece = -(-total // expert_count)
    spare = per_piece * expert_count - total
    packed = jnp.concatenate(tiles + [jnp.zeros((spare, SUB, LANE), jnp.bfloat16)], axis=0)
    packed = packed.reshape(expert_count, per_piece, SUB, LANE)
    packed, returned = lax.optimization_barrier((packed, returned))
    spread = lax.all_to_all(packed, "expert", split_axis=0, concat_axis=0, tiled=True)
    in_grad = lax.dot_general(
        select, returned, (((0,), (0,)), ((), ())), preferred_element_type=jnp.float32
    ).astype(jnp.bfloat16)
    picked = spread.at[partner].get(mode="promise_in_bounds")
    arrived = lax.all_to_all(picked, "expert", split_axis=0, concat_axis=0, tiled=True)
    arrived = arrived.reshape(-1, SUB, LANE)
    wide = (jnp.bfloat16, jnp.float32, jnp.float32)
    new_gu, gate_mean, gate_square, new_dn, down_mean, down_square = unpack_tiles(
        arrived, [u.shape for u in updated], wide + wide
    )
    return (
        in_grad,
        new_gu[None],
        new_dn[None],
        gate_mean[None],
        gate_square[None],
        down_mean[None],
        down_square[None],
    )


def solution(mesh):
    in_specs = (
        P(("dp", "expert"), None),
        P(("dp", "expert"), None),
        P(("dp", "expert"), None),
        P(("dp", "expert"), None),
        P("expert", None, None),
        P("expert", None, None),
        P("expert", "dp", None),
        P("expert", "dp", None),
        P("expert", None, "dp"),
        P("expert", None, "dp"),
        P(),
    )
    out_specs = (
        P(("dp", "expert"), None),
        P("expert", "dp", None),
        P("expert", None, "dp"),
        P("expert", "dp", None),
        P("expert", "dp", None),
        P("expert", None, "dp"),
        P("expert", None, "dp"),
    )
    return jax.shard_map(
        per_device, mesh=mesh, in_specs=in_specs, out_specs=out_specs, check_vma=False
    )
```

```python
import functools

import jax
import jax.numpy as jnp
from jax import lax
from jax.experimental import pallas as pl
from jax.experimental.pallas import tpu as pltpu
from jax.sharding import PartitionSpec as P

BETA_ONE = 0.9
BETA_TWO = 0.95
RATE = 0.001
DECAY = 0.1
ADAM_EPS = 1e-08
PEAK_EPS = 1e-06
SUB = 8
LANE = 128
PLANE = 16


def partner_table(swap_pairs, expert_count):
    devices = jnp.arange(expert_count, dtype=jnp.int32)
    first_dev = swap_pairs[:, 0]
    second_dev = swap_pairs[:, 1]
    hit_first = devices[:, None] == first_dev[None, :]
    hit_second = devices[:, None] == second_dev[None, :]
    other = jnp.sum(
        jnp.where(hit_first, second_dev[None, :], 0) + jnp.where(hit_second, first_dev[None, :], 0),
        axis=1,
    )
    paired = jnp.any(hit_first | hit_second, axis=1)
    return jnp.where(paired, other, devices)


def home_select(routes, expert_count, capacity):
    tok_rows = routes.shape[0]
    experts = jnp.arange(expert_count, dtype=jnp.int32)
    member = jnp.any(routes[:, :, None] == experts[None, None, :], axis=1)
    earlier = jnp.tril(jnp.ones((tok_rows, tok_rows), jnp.bfloat16), -1)
    rank = jnp.dot(earlier, member.astype(jnp.bfloat16), preferred_element_type=jnp.float32)
    place = jnp.where(member, rank.astype(jnp.int32), -1)
    slots = jnp.arange(capacity, dtype=jnp.int32)
    chosen = place.T[:, None, :] == slots[None, :, None]
    return chosen.astype(jnp.bfloat16).reshape(expert_count * capacity, tok_rows)


def column_select(routes, combine, first_expert, plane, sources, capacity):
    top_count, columns = routes.shape
    tok_rows = columns // sources
    wanted = first_expert + jnp.arange(plane, dtype=jnp.int32)
    hit = routes[:, None, :] == wanted[None, :, None]
    member = jnp.any(hit, axis=0)
    weight = jnp.sum(jnp.where(hit, combine[:, None, :], jnp.float32(0.0)), axis=0)
    column = jnp.arange(columns, dtype=jnp.int32)
    source = column // tok_rows
    earlier = (column[:, None] < column[None, :]) & (source[:, None] == source[None, :])
    rank = jnp.dot(
        member.astype(jnp.bfloat16),
        earlier.astype(jnp.bfloat16),
        preferred_element_type=jnp.float32,
    )
    code = jnp.where(member, source[None, :] * capacity + rank.astype(jnp.int32), -1)
    slots = jnp.arange(sources * capacity, dtype=jnp.int32)
    chosen = code[:, None, :] == slots[None, :, None]
    slot_weight = jnp.sum(jnp.where(chosen, weight[:, None, :], jnp.float32(0.0)), axis=2)
    select = chosen.astype(jnp.bfloat16).reshape(plane * sources * capacity, columns)
    return select, slot_weight.reshape(-1)


def ring_kernel(depth, plane, count, *refs):
    ins = refs[:count]
    outs = refs[count : 2 * count]
    send_sem, recv_sem = refs[2 * count :]
    me = lax.axis_index("expert")
    layer = me // plane
    spot = me % plane
    ahead = ((layer + 1) % depth) * plane + spot
    behind = ((layer + depth - 1) % depth) * plane + spot
    targets = (ahead, behind)

    barrier = pltpu.get_barrier_semaphore()
    for target in targets:
        pl.semaphore_signal(
            barrier, inc=1, device_id={"expert": target}, device_id_type=pl.DeviceIdType.MESH
        )
    pl.semaphore_wait(barrier, 2)

    half = depth // 2

    def copy_of(way, step, which, part):
        if way == 0:
            block = (layer + depth - step) % depth
        else:
            block = (layer + step) % depth
        rows = ins[which].shape[0] // 2
        some = pl.ds(part * rows, rows)
        source = ins[which].at[some] if step == 0 else outs[which].at[block, some]
        return pltpu.make_async_remote_copy(
            src_ref=source,
            dst_ref=outs[which].at[block, some],
            send_sem=send_sem.at[way, step, which, part],
            recv_sem=recv_sem.at[way, step, which, part],
            device_id={"expert": targets[way]},
            device_id_type=pl.DeviceIdType.MESH,
        )

    started = []
    previous = {}
    for step in range(half):
        for which in range(count):
            for part in (0, 1):
                for way in (0, 1):
                    if step == half - 1 and way != part:
                        continue
                    if step > 0:
                        previous.pop((way, which, part)).wait_recv()
                    copy = copy_of(way, step, which, part)
                    copy.start()
                    started.append(copy)
                    previous[(way, which, part)] = copy
        if step == 0:
            for which in range(count):
                outs[which][layer] = ins[which][...]
    for copy in previous.values():
        copy.wait_recv()
    for copy in started:
        copy.wait_send()


def gather_column(arrays, depth, plane, collective_id):
    half = depth // 2
    count = len(arrays)
    moved = sum(a.size * a.dtype.itemsize for a in arrays) * depth
    return pl.pallas_call(
        functools.partial(ring_kernel, depth, plane, count),
        out_shape=[jax.ShapeDtypeStruct((depth,) + a.shape, a.dtype) for a in arrays],
        in_specs=[pl.BlockSpec(memory_space=pltpu.VMEM)] * count,
        out_specs=[pl.BlockSpec(memory_space=pltpu.VMEM)] * count,
        scratch_shapes=[
            pltpu.SemaphoreType.DMA((2, half, count, 2)),
            pltpu.SemaphoreType.DMA((2, half, count, 2)),
        ],
        compiler_params=pltpu.CompilerParams(
            collective_id=collective_id,
            has_side_effects=True,
            vmem_limit_bytes=16 * 1024 * 1024,
        ),
        cost_estimate=pl.CostEstimate(flops=0, bytes_accessed=40 * moved, transcendentals=0),
    )(*arrays)


UNPACK_STEPS = 8


def unpack_kernel(*refs):
    for tiles, out in zip(refs[:6], refs[6:]):
        cols = out.shape[1] // LANE
        for group in range(out.shape[0] // SUB):
            for col in range(cols):
                out[group * SUB : (group + 1) * SUB, col * LANE : (col + 1) * LANE] = tiles[
                    group * cols + col
                ].astype(out.dtype)


def unpack_tiles(arrived, shapes, dtypes):
    in_specs = []
    out_specs = []
    start = 0
    for rows, cols in shapes:
        count = rows * cols // (SUB * LANE)
        block = count // UNPACK_STEPS
        first = start // block
        in_specs.append(
            pl.BlockSpec((block, SUB, LANE), functools.partial(lambda b, i: (b + i, 0, 0), first))
        )
        out_specs.append(pl.BlockSpec((rows // UNPACK_STEPS, cols), lambda i: (i, 0)))
        start += count
    return pl.pallas_call(
        unpack_kernel,
        grid=(UNPACK_STEPS,),
        out_shape=[jax.ShapeDtypeStruct(s, d) for s, d in zip(shapes, dtypes)],
        in_specs=in_specs,
        out_specs=out_specs,
    )(*([arrived] * 6))


def to_tiles(matrix):
    rows, cols = matrix.shape
    tiles = matrix.reshape(rows // SUB, SUB, cols // LANE, LANE).transpose(0, 2, 1, 3)
    return tiles.reshape(-1, SUB, LANE)


def adam_update(weight, grad, mean_in, square_in, scale_by):
    scaled = grad * scale_by
    mean_new = BETA_ONE * mean_in + (1.0 - BETA_ONE) * scaled
    square_new = BETA_TWO * square_in + (1.0 - BETA_TWO) * scaled * scaled
    weight_wide = weight.astype(jnp.float32)
    step_size = mean_new / (jnp.sqrt(square_new) + ADAM_EPS)
    weight_new = weight_wide - RATE * (step_size + DECAY * weight_wide)
    return (
        weight_new.astype(jnp.bfloat16),
        mean_new.astype(jnp.bfloat16),
        square_new.astype(jnp.bfloat16),
    )


def per_device(
    out_grad,
    layer_input,
    combine,
    routes,
    w_gate_up,
    w_down,
    m_gate_up,
    v_gate_up,
    m_down,
    v_down,
    swap_pairs,
):
    expert_count = lax.axis_size("expert")
    replicas = lax.axis_size("dp")
    replica = lax.axis_index("dp")
    partner = partner_table(swap_pairs, expert_count)
    tok_rows, top_count = routes.shape
    capacity = 2 * tok_rows * top_count // expert_count
    model_width = out_grad.shape[1]
    gate_up = w_gate_up[0]
    down_proj = w_down[0]
    hidden_units = down_proj.shape[0]

    def swap_tokens(rows):
        return lax.all_to_all(
            rows.reshape(expert_count, capacity, model_width),
            "expert",
            split_axis=0,
            concat_axis=0,
            tiled=True,
        ).reshape(expert_count * capacity, model_width)

    plane = PLANE
    depth = expert_count // plane
    layer = lax.axis_index("expert") // plane
    groups = [[z * plane + spot for spot in range(plane)] for z in range(depth)]

    def send_in_plane(rows):
        return lax.all_to_all(
            rows.reshape(plane, depth * capacity, model_width),
            "expert",
            split_axis=0,
            concat_axis=0,
            axis_index_groups=groups,
            tiled=True,
        ).reshape(expert_count * capacity, model_width)

    notes = jnp.concatenate([routes.T.astype(jnp.float32), combine.T], axis=0)
    notes = jnp.pad(notes, ((0, 0), (0, LANE - tok_rows)))
    all_notes, all_input = gather_column((notes, layer_input), depth, plane, 0)
    all_notes = all_notes[:, :, :tok_rows].transpose(1, 0, 2).reshape(2 * top_count, -1)
    column_routes = all_notes[:top_count].astype(jnp.int32)
    pick, slot_weight = column_select(
        column_routes, all_notes[top_count:], layer * plane, plane, depth, capacity
    )
    slot_input = jnp.dot(
        pick, all_input.reshape(-1, model_width), preferred_element_type=jnp.float32
    ).astype(jnp.bfloat16)
    slot_input, out_grad = lax.optimization_barrier((slot_input, out_grad))
    slot_input = send_in_plane(slot_input)
    (all_grad,) = gather_column((out_grad,), depth, plane, 1)
    slot_grad = (
        jnp.dot(pick, all_grad.reshape(-1, model_width), preferred_element_type=jnp.float32)
        * slot_weight[:, None]
    ).astype(jnp.bfloat16)
    slot_grad = send_in_plane(slot_grad)
    select = home_select(routes, expert_count, capacity)

    pre_act = jnp.dot(slot_input, gate_up, preferred_element_type=jnp.float32)
    gate_pre = pre_act[:, :hidden_units]
    up_pre = pre_act[:, hidden_units:]
    sigmoid_gate = jax.nn.sigmoid(gate_pre)
    gate_act = gate_pre * sigmoid_gate
    hidden = (gate_act * up_pre).astype(jnp.bfloat16)
    d_hidden = lax.dot_general(
        slot_grad, down_proj, (((1,), (1,)), ((), ())), preferred_element_type=jnp.float32
    )
    d_gate = d_hidden * up_pre * sigmoid_gate * (1.0 + gate_pre * (1.0 - sigmoid_gate))
    d_up = d_hidden * gate_act
    d_pre = jnp.concatenate([d_gate, d_up], axis=1).astype(jnp.bfloat16)
    slot_back = lax.dot_general(
        d_pre, gate_up, (((1,), (1,)), ((), ())), preferred_element_type=jnp.float32
    ).astype(jnp.bfloat16)
    slot_back, d_pre, hidden = lax.optimization_barrier((slot_back, d_pre, hidden))
    by_home = slot_back.reshape(plane, depth, capacity, model_width).transpose(1, 0, 2, 3)
    returned = swap_tokens(by_home)

    grad_down = lax.dot_general(
        hidden, slot_grad, (((0,), (0,)), ((), ())), preferred_element_type=jnp.float32
    )
    grad_gate_up = lax.dot_general(
        slot_input, d_pre, (((0,), (0,)), ((), ())), preferred_element_type=jnp.float32
    )
    half = model_width // replicas
    mine = replica * half
    other = (1 - replica) * half
    trade = [(0, 1), (1, 0)]
    sent_gate_up = lax.dynamic_slice_in_dim(grad_gate_up, other, half, 0).astype(jnp.bfloat16)
    sent_down = lax.dynamic_slice_in_dim(grad_down, other, half, 1).astype(jnp.bfloat16)
    part_gate_up = lax.dynamic_slice_in_dim(grad_gate_up, mine, half, 0) + lax.ppermute(
        sent_gate_up, "dp", trade
    ).astype(jnp.float32)
    part_down = lax.dynamic_slice_in_dim(grad_down, mine, half, 1) + lax.ppermute(
        sent_down, "dp", trade
    ).astype(jnp.float32)
    local_peak = jnp.maximum(jnp.max(jnp.abs(part_gate_up)), jnp.max(jnp.abs(part_down)))
    peak_abs = lax.pmax(local_peak, "dp")
    scale_by = 1.0 / (peak_abs + PEAK_EPS)
    own_gate_up = lax.dynamic_slice_in_dim(gate_up, mine, half, 0)
    own_down = lax.dynamic_slice_in_dim(down_proj, mine, half, 1)
    updated = adam_update(own_gate_up, part_gate_up, m_gate_up[0], v_gate_up[0], scale_by)
    updated += adam_update(own_down, part_down, m_down[0], v_down[0], scale_by)

    tiles = [to_tiles(u) for u in updated]
    counts = [t.shape[0] for t in tiles]
    total = sum(counts)
    per_piece = -(-total // expert_count)
    spare = per_piece * expert_count - total
    packed = jnp.concatenate(tiles + [jnp.zeros((spare, SUB, LANE), jnp.bfloat16)], axis=0)
    packed = packed.reshape(expert_count, per_piece, SUB, LANE)
    packed, returned = lax.optimization_barrier((packed, returned))
    spread = lax.all_to_all(packed, "expert", split_axis=0, concat_axis=0, tiled=True)
    in_grad = lax.dot_general(
        select, returned, (((0,), (0,)), ((), ())), preferred_element_type=jnp.float32
    ).astype(jnp.bfloat16)
    picked = spread.at[partner].get(mode="promise_in_bounds")
    arrived = lax.all_to_all(picked, "expert", split_axis=0, concat_axis=0, tiled=True)
    arrived = arrived.reshape(-1, SUB, LANE)
    wide = (jnp.bfloat16, jnp.float32, jnp.float32)
    new_gu, gate_mean, gate_square, new_dn, down_mean, down_square = unpack_tiles(
        arrived, [u.shape for u in updated], wide + wide
    )
    return (
        in_grad,
        new_gu[None],
        new_dn[None],
        gate_mean[None],
        gate_square[None],
        down_mean[None],
        down_square[None],
    )


def solution(mesh):
    in_specs = (
        P(("dp", "expert"), None),
        P(("dp", "expert"), None),
        P(("dp", "expert"), None),
        P(("dp", "expert"), None),
        P("expert", None, None),
        P("expert", None, None),
        P("expert", "dp", None),
        P("expert", "dp", None),
        P("expert", None, "dp"),
        P("expert", None, "dp"),
        P(),
    )
    out_specs = (
        P(("dp", "expert"), None),
        P("expert", "dp", None),
        P("expert", None, "dp"),
        P("expert", "dp", None),
        P("expert", "dp", None),
        P("expert", None, "dp"),
        P("expert", None, "dp"),
    )
    return jax.shard_map(
        per_device, mesh=mesh, in_specs=in_specs, out_specs=out_specs, check_vma=False
    )
```
